32 devices in a mesh: row: 4 (over y, x), col: 8 (over z, core).
Axes of the slice: x: 2, y: 2, z: 4, core: 2. Of those that a mesh axis runs over, the one named last changes fastest.
Arguments:
- spectra: bfloat16 [8192, 2, 8, 256], P(('row', 'col')), may hold values from -6 to 6
- pair_grad: bfloat16 [4, 2048, 2, 8, 8192], P(None, 'col', None, None, 'row'), may hold values from -0.0625 to 0.0625
- assign: int32 [8192], replicated, may hold values from 0 to 8191, each once
- tile_mask: int32 [128, 128], replicated, may hold values 0 or 1
Outputs:
- spectra_grad: float32 [8192, 2, 8, 256], P(('row', 'col'))
The draws below stay inside these ranges and needn't reach their ends.
Inputs may be any that keep to these rules, and one draw needn't show every extreme that they name: `assign`: each number of 0 to 8191 appears once.
All inputs are finite; a program needn't handle non-finite values.
Results may differ from the reference program's by a relative error of at most 0.0003.
Values may be sent and summed in bfloat16 or wider, within the bound.
A program may use at most 384 MiB of HBM per device.

```python
import jax
import jax.numpy as jnp

CH = 8192
F = 8
W = 256
TILE = 64
NT = 128
RB = 2048
N_ROW = 4


def place_ends(values, stream_key, smallest, high):
    dims = values.shape
    index_at = [jax.random.randint(jax.random.fold_in(stream_key, axis), (), 0, dims[axis]) for axis in range(len(dims))]
    values = values.at[tuple(index_at)].set(smallest)
    longest = dims.index(max(dims))
    index_at[longest] = (index_at[longest] + 1) % dims[longest]
    return values.at[tuple(index_at)].set(high)


def level_of(stream_key, shape, shards, least, top_value):
    def one(axis_at, parts):
        draws = jax.random.uniform(jax.random.fold_in(jax.random.fold_in(stream_key, 6), axis_at), (parts,), jnp.float32, least / len(shards), top_value / len(shards))
        return jnp.repeat(jnp.exp(draws), shape[axis_at] // parts).reshape((-1,) + (1,) * (len(shape) - axis_at - 1))

    factor_of = one(*shards[0])
    for cut in shards[1:]:
        factor_of = factor_of * one(*cut)
    return factor_of


def gaussian(own_key, extent, width, bound, split=(), kind=jnp.bfloat16):
    level = level_of(own_key, extent, split, -0.22, 0.18) if split else 1.0
    result = jax.random.normal(own_key, extent, jnp.float32) * width * level
    return jnp.minimum(jnp.maximum(result, -bound), bound).astype(kind)


def setup_inputs(seed: int = 0) -> dict:
    key_of = jax.random.split(jax.random.key(seed), 5)
    return {
        "spectra": gaussian(key_of[0], (CH, 2, F, W), 1.0, 6.0, ((0, 32),)),
        "pair_grad": gaussian(key_of[1], (N_ROW, RB, 2, F, CH), CH ** -0.5, 0.0625, ((1, 8), (4, 4))),
        "assign": jax.random.permutation(key_of[2], CH).astype(jnp.int32),
        "tile_mask": place_ends((jax.random.randint(key_of[3], (NT, NT), 0, 4) < 3).astype(jnp.int32), jax.random.fold_in(key_of[3], 1), 0, 1),
    }


def reference(spectra, pair_grad, assign, tile_mask):
    channels = spectra.shape[0]
    grads = pair_grad.reshape(channels, 2, F, channels)
    places = jnp.arange(channels, dtype=jnp.int32)
    tile_of = places // TILE
    tile_rows = jnp.take(tile_mask, tile_of, axis=0)
    tile_grid = jnp.take(tile_rows, tile_of, axis=1)
    counted = (tile_grid == 1) & (assign[:, None] <= assign[None, :])
    counted_t = counted.T
    zero_value = jnp.zeros((), jnp.bfloat16)
    results = []
    for band_bin in range(F):
        real_g = jnp.where(counted_t, grads[:, 0, band_bin, :], zero_value)
        imag_g = jnp.where(counted_t, grads[:, 1, band_bin, :], zero_value)
        spec_real = spectra[:, 0, band_bin, :]
        spec_imag = spectra[:, 1, band_bin, :]
        real_t = real_g.T
        imag_t = imag_g.T
        row_real = jnp.dot(real_t, spec_real, preferred_element_type=jnp.float32) - jnp.dot(imag_t, spec_imag, preferred_element_type=jnp.float32)
        row_imag = jnp.dot(real_t, spec_imag, preferred_element_type=jnp.float32) + jnp.dot(imag_t, spec_real, preferred_element_type=jnp.float32)
        col_real = jnp.dot(real_g, spec_real, preferred_element_type=jnp.float32) + jnp.dot(imag_g, spec_imag, preferred_element_type=jnp.float32)
        col_imag = jnp.dot(real_g, spec_imag, preferred_element_type=jnp.float32) - jnp.dot(imag_g, spec_real, preferred_element_type=jnp.float32)
        results.append(jnp.stack([row_real + col_real, row_imag + col_imag], axis=1))
    return jnp.stack(results, axis=2)
```

```python
import jax
import jax.numpy as jnp
from jax import lax
from jax.experimental.layout import Layout, with_layout_constraint
from jax.sharding import PartitionSpec as P

TILE = 64
CHUNKS = 2
SCALE = 8.0


def pick(x, index, axis):
    return lax.dynamic_index_in_dim(x, index, axis, keepdims=False)


def swap_cores(x, n_col):
    return lax.ppermute(x, "col", [(i, i ^ 1) for i in range(n_col)])


def line_perm(sources, step, n_col):
    line = n_col // 2
    return [
        (z * 2 + core, (z + step) * 2 + core)
        for z in sources
        for core in range(2)
        if 0 <= z + step < line
    ]


def major(x):
    return with_layout_constraint(x, Layout(major_to_minor=tuple(range(x.ndim))))


def both(spec, sign):
    width = spec.shape[-1] // 2
    one, none = jnp.eye(width, dtype=spec.dtype), jnp.zeros((width, width), spec.dtype)
    same = jnp.block([[one, none], [none, one]])
    turn = jnp.block([[none, sign * one], [-sign * one, none]]).astype(spec.dtype)
    return jnp.einsum("fin,cnm->cfim", spec, jnp.stack([same, turn]), preferred_element_type=spec.dtype)


def gather_line(block, z, core, n_col):
    line = n_col // 2
    to_right, to_left = [block], [block]
    for step in range(line - 1):
        to_right.append(lax.ppermute(to_right[-1], "col", line_perm(range(step, line), 1, n_col)))
        to_left.append(lax.ppermute(to_left[-1], "col", line_perm(range(line - step), -1, n_col)))
    held = major(jnp.zeros(block.shape[:1] + (n_col,) + block.shape[1:], block.dtype))
    for step in range(line):
        got = block if step == 0 else jnp.where(z >= step, to_right[step], to_left[line - step])
        source = lax.rem(z - step + line, line) * 2
        held = lax.dynamic_update_slice(held, got[:, None], (0, source + core, 0, 0))
        other = swap_cores(got, n_col)
        held = lax.dynamic_update_slice(held, other[:, None], (0, source + 1 - core, 0, 0))
    return major(held).reshape(block.shape[0], -1, block.shape[-1])


def gather_cube(block, row, n_row, bits):
    parts = [(0, block)]
    for bit in bits:
        perm = [(i, i ^ (1 << bit)) for i in range(n_row)]
        parts = parts + [(far | (1 << bit), lax.ppermute(x, "row", perm)) for far, x in parts]
    held = major(jnp.zeros(block.shape[:1] + (n_row,) + block.shape[1:], block.dtype))
    for far, x in parts:
        held = lax.dynamic_update_slice(held, x[:, None], (0, row ^ far, 0, 0))
    return major(held).reshape(block.shape[0], -1, block.shape[-1])


def after(x, *others):
    return lax.optimization_barrier((x,) + others)


class LineSum:
    def __init__(self, part, z, core, n_col):
        bins, rows, cols = part.shape
        self.z, self.core, self.n_col, self.line = z, core, n_col, n_col // 2
        part = part.reshape(bins, self.line, 2, rows // n_col, cols)
        self.keep = pick(part, core, 2)
        self.swapped = swap_cores(pick(part, 1 - core, 2), n_col)
        self.right = self.left = None
        self.step = 0

    def encode(self):
        if self.step == 0:
            self.chip = self.keep + self.swapped
        self.step += 1
        right = pick(self.chip, jnp.clip(self.line - self.step + self.z, 0, self.line - 1), 1)
        left = pick(self.chip, jnp.clip(self.step - self.line + self.z, 0, self.line - 1), 1)
        if self.step > 1:
            right, left = right + self.right, left + self.left
        self.out = [(x * SCALE).astype(jnp.float16) for x in (right, left)]

    def send(self):
        line, step, n_col = self.line, self.step, self.n_col
        right = lax.ppermute(self.out[0], "col", line_perm(range(step), 1, n_col))
        left = lax.ppermute(self.out[1], "col", line_perm(range(line - step, line), -1, n_col))
        self.right, self.left = [x.astype(jnp.float32) * (1.0 / SCALE) for x in (right, left)]

    def total(self):
        while self.step < self.line - 1:
            self.encode()
            self.send()
        return pick(self.chip, self.z, 1) + self.right + self.left


def reduce_cube(part, row, n_row, bits):
    bins, rows, cols = part.shape
    part = part.reshape((bins,) + (2,) * len(bits) + (rows // n_row, cols))
    left = sorted(bits, reverse=True)
    for bit in bits:
        axis = 1 + left.index(bit)
        high = (row >> bit) & 1
        perm = [(i, i ^ (1 << bit)) for i in range(n_row)]
        part = pick(part, high, axis) + lax.ppermute(pick(part, 1 - high, axis), "row", perm)
        left.remove(bit)
    return part


def make_body(n_row, n_col):
    def body(spectra, pair_grad, assign, tile_mask):
        row = lax.axis_index("row")
        col = lax.axis_index("col")
        z, core = col // 2, col % 2
        blocks, width_b, _, bins, block_p = pair_grad.shape
        cube_bits = list(range(n_row.bit_length() - 1))
        per = bins // CHUNKS
        own = jnp.concatenate([jnp.swapaxes(spectra[:, d], 0, 1) for d in range(2)], axis=-1)
        pieces = [major(own[k * per : (k + 1) * per]) for k in range(CHUNKS)]
        orders = [cube_bits[:: (-1) ** k] for k in range(CHUNKS)]
        col_specs = [gather_cube(x, row, n_row, bits) for x, bits in zip(pieces, orders)]
        row_specs = [gather_line(x, z, core, n_col) for x in pieces]

        p_owner = lax.dynamic_slice_in_dim(assign, row * block_p, block_p)
        q_owner = pick(assign.reshape(blocks, n_col, width_b), col, 1).reshape(-1)
        tiles = lax.dynamic_slice_in_dim(tile_mask, row * (block_p // TILE), block_p // TILE, axis=0)
        tiles = pick(tiles.reshape(block_p // TILE, blocks, n_col, width_b // TILE), col, 2)
        tiles = tiles.reshape(block_p // TILE, -1).T
        grid = jnp.repeat(jnp.repeat(tiles, TILE, axis=1), TILE, axis=0)
        counted = (grid == 1) & (p_owner[None, :] <= q_owner[:, None])

        grads = pair_grad.reshape(blocks * width_b, 2, bins, block_p)
        grads = jnp.transpose(grads, (1, 2, 0, 3))
        masked = [
            jnp.where(counted, grads[:, k * per : (k + 1) * per], jnp.zeros((), jnp.bfloat16))
            for k in range(CHUNKS)
        ]
        sums = []
        for k in range(CHUNKS):
            row_part = jnp.einsum(
                "cfqp,cfqn->fpn", masked[k], both(col_specs[k], 1), preferred_element_type=jnp.float32
            )
            sums.append(LineSum(row_part, z, core, n_col))
        outs = []
        for k in range(CHUNKS):
            ready = []
            for line_sum in sums[: k + 1]:
                if line_sum.step < line_sum.line - 1:
                    line_sum.encode()
                    ready.append(line_sum)
            sent = [x for line_sum in ready for x in line_sum.out]
            spec, *sent = after(row_specs[k], *sent)
            for i, line_sum in enumerate(ready):
                line_sum.out = sent[2 * i : 2 * i + 2]
                line_sum.send()
            col_part = jnp.einsum(
                "cfqp,cfpn->fqn", masked[k], both(spec, -1), preferred_element_type=jnp.float32
            )
            outs.append(reduce_cube(col_part, row, n_row, orders[k]))
        totals = [x + line_sum.total() for x, line_sum in zip(outs, sums)]
        width = spectra.shape[3]
        halves = [
            jnp.concatenate([x[:, :, d * width : (d + 1) * width] for x in totals], axis=0) for d in range(2)
        ]
        return jnp.transpose(major(jnp.stack(halves, axis=0)), (2, 0, 1, 3))

    return body


def solution(mesh):
    return jax.shard_map(
        make_body(mesh.shape["row"], mesh.shape["col"]),
        mesh=mesh,
        in_specs=(P(("row", "col"), None, None, None), P(None, "col", None, None, "row"), P(), P()),
        out_specs=P(("row", "col"), None, None, None),
        check_vma=False,
    )
```

```python
import jax
import jax.numpy as jnp
from jax import lax
from jax.experimental.layout import Layout, with_layout_constraint
from jax.sharding import PartitionSpec as P

TILE = 64
CHUNKS = 2
SCALE = 8.0


def pick(x, index, axis):
    return lax.dynamic_index_in_dim(x, index, axis, keepdims=False)


def swap_cores(x, n_col):
    return lax.ppermute(x, "col", [(i, i ^ 1) for i in range(n_col)])


def line_perm(sources, step, n_col):
    line = n_col // 2
    return [
        (z * 2 + core, (z + step) * 2 + core)
        for z in sources
        for core in range(2)
        if 0 <= z + step < line
    ]


def major(x):
    return with_layout_constraint(x, Layout(major_to_minor=tuple(range(x.ndim))))


def both(spec, sign):
    width = spec.shape[-1] // 2
    one, none = jnp.eye(width, dtype=spec.dtype), jnp.zeros((width, width), spec.dtype)
    same = jnp.block([[one, none], [none, one]])
    turn = jnp.block([[none, sign * one], [-sign * one, none]]).astype(spec.dtype)
    return jnp.einsum("fin,cnm->cfim", spec, jnp.stack([same, turn]), preferred_element_type=spec.dtype)


def gather_line(block, z, core, n_col):
    line = n_col // 2
    to_right, to_left = [block], [block]
    for step in range(line - 1):
        to_right.append(lax.ppermute(to_right[-1], "col", line_perm(range(step, line), 1, n_col)))
        to_left.append(lax.ppermute(to_left[-1], "col", line_perm(range(line - step), -1, n_col)))
    held = major(jnp.zeros(block.shape[:1] + (n_col,) + block.shape[1:], block.dtype))
    for step in range(line):
        got = block if step == 0 else jnp.where(z >= step, to_right[step], to_left[line - step])
        source = lax.rem(z - step + line, line) * 2
        held = lax.dynamic_update_slice(held, got[:, None], (0, source + core, 0, 0))
        other = swap_cores(got, n_col)
        held = lax.dynamic_update_slice(held, other[:, None], (0, source + 1 - core, 0, 0))
    return major(held).reshape(block.shape[0], -1, block.shape[-1])


def gather_cube(block, row, n_row, bits):
    parts = [(0, block)]
    for bit in bits:
        perm = [(i, i ^ (1 << bit)) for i in range(n_row)]
        parts = parts + [(far | (1 << bit), lax.ppermute(x, "row", perm)) for far, x in parts]
    held = major(jnp.zeros(block.shape[:1] + (n_row,) + block.shape[1:], block.dtype))
    for far, x in parts:
        held = lax.dynamic_update_slice(held, x[:, None], (0, row ^ far, 0, 0))
    return major(held).reshape(block.shape[0], -1, block.shape[-1])


def after(x, *others):
    return lax.optimization_barrier((x,) + others)


class LineSum:
    def __init__(self, part, z, core, n_col):
        bins, rows, cols = part.shape
        self.z, self.core, self.n_col, self.line = z, core, n_col, n_col // 2
        part = part.reshape(bins, self.line, 2, rows // n_col, cols)
        self.keep = pick(part, core, 2)
        self.swapped = swap_cores(pick(part, 1 - core, 2), n_col)
        self.right = self.left = None
        self.step = 0

    def encode(self):
        if self.step == 0:
            self.chip = self.keep + self.swapped
        self.step += 1
        right = pick(self.chip, jnp.clip(self.line - self.step + self.z, 0, self.line - 1), 1)
        left = pick(self.chip, jnp.clip(self.step - self.line + self.z, 0, self.line - 1), 1)
        if self.step > 1:
            right, left = right + self.right, left + self.left
        self.out = [(x * SCALE).astype(jnp.float16) for x in (right, left)]

    def send(self):
        line, step, n_col = self.line, self.step, self.n_col
        right = lax.ppermute(self.out[0], "col", line_perm(range(step), 1, n_col))
        left = lax.ppermute(self.out[1], "col", line_perm(range(line - step, line), -1, n_col))
        self.right, self.left = [x.astype(jnp.float32) * (1.0 / SCALE) for x in (right, left)]

    def total(self):
        while self.step < self.line - 1:
            self.encode()
            self.send()
        return pick(self.chip, self.z, 1) + self.right + self.left


def reduce_cube(part, row, n_row, bits):
    bins, rows, cols = part.shape
    part = part.reshape((bins,) + (2,) * len(bits) + (rows // n_row, cols))
    left = sorted(bits, reverse=True)
    for bit in bits:
        axis = 1 + left.index(bit)
        high = (row >> bit) & 1
        perm = [(i, i ^ (1 << bit)) for i in range(n_row)]
        part = pick(part, high, axis) + lax.ppermute(pick(part, 1 - high, axis), "row", perm)
        left.remove(bit)
    return part


def make_body(n_row, n_col):
    def body(spectra, pair_grad, assign, tile_mask):
        row = lax.axis_index("row")
        col = lax.axis_index("col")
        z, core = col // 2, col % 2
        blocks, width_b, _, bins, block_p = pair_grad.shape
        cube_bits = list(range(n_row.bit_length() - 1))
        per = bins // CHUNKS
        own = jnp.concatenate([jnp.swapaxes(spectra[:, d], 0, 1) for d in range(2)], axis=-1)
        pieces = [major(own[k * per : (k + 1) * per]) for k in range(CHUNKS)]
        orders = [cube_bits[:: (-1) ** k] for k in range(CHUNKS)]
        col_specs = [gather_cube(x, row, n_row, bits) for x, bits in zip(pieces, orders)]
        row_specs = [gather_line(x, z, core, n_col) for x in pieces]

        p_owner = lax.dynamic_slice_in_dim(assign, row * block_p, block_p)
        q_owner = pick(assign.reshape(blocks, n_col, width_b), col, 1).reshape(-1)
        tiles = lax.dynamic_slice_in_dim(tile_mask, row * (block_p // TILE), block_p // TILE, axis=0)
        tiles = pick(tiles.reshape(block_p // TILE, blocks, n_col, width_b // TILE), col, 2)
        tiles = tiles.reshape(block_p // TILE, -1).T
        grid = jnp.repeat(jnp.repeat(tiles, TILE, axis=1), TILE, axis=0)
        counted = (grid == 1) & (p_owner[None, :] <= q_owner[:, None])

        grads = pair_grad.reshape(blocks * width_b, 2, bins, block_p)
        grads = jnp.transpose(grads, (1, 2, 0, 3))
        masked = [
            jnp.where(counted, grads[:, k * per : (k + 1) * per], jnp.zeros((), jnp.bfloat16))
            for k in range(CHUNKS)
        ]
        sums = []
        for k in range(CHUNKS):
            row_part = jnp.einsum(
                "cfqp,cfqn->fpn", masked[k], both(col_specs[k], 1), preferred_element_type=jnp.float32
            )
            sums.append(LineSum(row_part, z, core, n_col))
        outs = []
        for k in range(CHUNKS):
            ready = []
            for line_sum in sums[: k + 1]:
                if line_sum.step < line_sum.line - 1:
                    line_sum.encode()
                    ready.append(line_sum)
            sent = [x for line_sum in ready for x in line_sum.out]
            spec, *sent = after(row_specs[k], *sent)
            for i, line_sum in enumerate(ready):
                line_sum.out = sent[2 * i : 2 * i + 2]
                line_sum.send()
            spec = both(spec, -1)
            if len(ready) > 1:
                early = ready[0]
                spec, early.right, early.left = after(spec, early.right, early.left)
            col_part = jnp.einsum(
                "cfqp,cfpn->fqn", masked[k], spec, preferred_element_type=jnp.float32
            )
            outs.append(reduce_cube(col_part, row, n_row, orders[k]))
        totals = [x + line_sum.total() for x, line_sum in zip(outs, sums)]
        width = spectra.shape[3]
        halves = [
            jnp.concatenate([x[:, :, d * width : (d + 1) * width] for x in totals], axis=0) for d in range(2)
        ]
        return jnp.transpose(major(jnp.stack(halves, axis=0)), (2, 0, 1, 3))

    return body


def solution(mesh):
    return jax.shard_map(
        make_body(mesh.shape["row"], mesh.shape["col"]),
        mesh=mesh,
        in_specs=(P(("row", "col"), None, None, None), P(None, "col", None, None, "row"), P(), P()),
        out_specs=P(("row", "col"), None, None, None),
        check_vma=False,
    )
```
